32 devices in a mesh: gx: 4 (over z), gy: 8 (over y, x, core).
Axes of the slice: x: 2, y: 2, z: 4, core: 2. Of those that a mesh axis runs over, the one named last changes fastest.
Arguments:
- source: float32 [128, 256, 128], P('gx', 'gy'), may hold values from -6 to 6
- inverse_density: float32 [128, 256, 128], P('gx', 'gy'), may hold values from 1 to 7
Outputs:
- correction: float32 [128, 256, 128], P('gx', 'gy')
The draws below stay inside these ranges and needn't reach their ends.
All inputs are finite; a program needn't handle non-finite values.
Results may differ from the reference program's by a relative error of at most 0.0001.
Values sent between devices are 32-bit elements; how exact they have to be, the bound alone decides.
A program may use at most 128 MiB of HBM per device.

```python
import math
import jax
import jax.numpy as jnp

NZ = 128
LEVELS = 4
NU1 = 3
NU2 = 2
NC = 5
NX = 128
NY = 256


def draw_source(key, part):
    extent = (NX, NY, NZ)
    return jnp.clip(jax.random.normal(key, extent, jnp.float32), -6.0, 6.0)


def block_scale(key, dims, split, smallest, top_value):
    def one(dim, parts):
        steps = jax.random.uniform(jax.random.fold_in(jax.random.fold_in(key, 6), dim), (parts,), jnp.float32, smallest / len(split), top_value / len(split))
        return jnp.repeat(jnp.exp(steps), dims[dim] // parts).reshape((-1,) + (1,) * (len(dims) - dim - 1))

    level = one(*split[0])
    for cut in split[1:]:
        level = level * one(*cut)
    return level


def setup_inputs(seed: int = 0) -> dict:
    key_list = jax.random.split(jax.random.key(seed), 3)
    return {
        "source": draw_source(jax.random.fold_in(key_list[2], 71), 0),
        "inverse_density": jnp.clip(jnp.exp(math.log(7.0) - 1.9459101 * jax.random.uniform(key_list[1], (NX, NY, NZ), jnp.float32) ** block_scale(key_list[1], (NX, NY, NZ), ((0, 4), (1, 8)), -0.2, 0.2)), 1.0, 7.0),
    }


OMEGA = 0.8


def harmonic(left_value, right_value):
    return 2.0 * left_value * right_value / (left_value + right_value)


def centre_and_others(padded):
    centre = padded[1:-1, 1:-1, 1:-1]
    others = [padded[:-2, 1:-1, 1:-1], padded[2:, 1:-1, 1:-1], padded[1:-1, :-2, 1:-1],
              padded[1:-1, 2:, 1:-1], padded[1:-1, 1:-1, :-2], padded[1:-1, 1:-1, 2:]]
    return centre, others


def coefficients(coef_padded, factor):
    centre, others = centre_and_others(coef_padded)
    couplings = [factor * harmonic(centre, neighbour) for neighbour in others]
    diagonal = couplings[0] + couplings[1] + couplings[2] + couplings[3] + couplings[4] + couplings[5]
    return couplings, diagonal


def residual_of(field_padded, source, couplings):
    centre, others = centre_and_others(field_padded)
    applied = couplings[0] * (centre - others[0])
    for position in range(1, 6):
        applied = applied + couplings[position] * (centre - others[position])
    return source - applied


def pad_depth(values, replicate_ends):
    if replicate_ends:
        return jnp.concatenate([values[:, :, :1], values, values[:, :, -1:]], axis=2)
    zero_layer = jnp.zeros(values.shape[:2] + (1,), jnp.float32)
    return jnp.concatenate([zero_layer, values, zero_layer], axis=2)


def wrap_rims(values, replicate_ends):
    widened = jnp.pad(values, ((1, 1), (1, 1), (0, 0)), mode="wrap")
    return pad_depth(widened, replicate_ends)


def restrict(values):
    extent = values.shape
    return jnp.mean(values.reshape(extent[0] // 2, 2, extent[1] // 2, 2, extent[2] // 2, 2), axis=(1, 3, 5))


def prolong(values):
    return jnp.repeat(jnp.repeat(jnp.repeat(values, 2, axis=0), 2, axis=1), 2, axis=2)


def reference(source, inverse_density):
    records = []
    current_source, current_beta = source, inverse_density
    for level_number in range(LEVELS):
        factor = 0.25 ** level_number
        couplings, diagonal = coefficients(wrap_rims(current_beta, True), factor)
        sweeps = NC if level_number == LEVELS - 1 else NU1
        iterate = OMEGA * current_source / diagonal
        for sweep_number in range(sweeps - 1):
            iterate = iterate + OMEGA * residual_of(wrap_rims(iterate, False), current_source, couplings) / diagonal
        records.append((iterate, current_source, couplings, diagonal))
        if level_number < LEVELS - 1:
            residual = residual_of(wrap_rims(iterate, False), current_source, couplings)
            current_source = restrict(residual)
            current_beta = restrict(current_beta)
    correction = records[LEVELS - 1][0]
    for level_number in range(LEVELS - 2, -1, -1):
        iterate, level_source, couplings, diagonal = records[level_number]
        iterate = iterate + prolong(correction)
        for sweep_number in range(NU2):
            iterate = iterate + OMEGA * residual_of(wrap_rims(iterate, False), level_source, couplings) / diagonal
        correction = iterate
    return correction
```

```python
import functools

import jax
import jax.numpy as jnp
from jax import lax
from jax.experimental import pallas as pl
from jax.experimental.pallas import tpu as pltpu
from jax.sharding import PartitionSpec as P

MESH = pl.DeviceIdType.MESH
OMEGA = 0.8
F32 = jnp.float32

PLANES = (42, 16, 12, 5)
ROWS = (48, 40, 48, 32)
AT = (5, 6, 16, 8)
SPAN = ((1, 40), (2, 24), (1, 40), (2, 16))
BUILD = ((1, 40), (1, 32), (1, 40), (2, 16))
OWN = 32
NEAR = [(dx, dy) for dx in (1, -1, 0) for dy in (0, 1, -1) if (dx, dy) != (0, 0)]


def far_offsets(peers):
    return (-1, 0, 1, 2) if peers == 4 else (-2, -1, 0, 1, 2)


def lanes(value, shift):
    return pltpu.roll(value, shift % 128, 1)


def rows(value, shift):
    return pltpu.roll(value, shift % value.shape[0], 0)


def lane_index(height):
    return lax.broadcasted_iota(jnp.int32, (height, 128), 1)


def swap_lanes(value, step):
    low = (lane_index(value.shape[0]) & step) == 0
    return jnp.where(low, lanes(value, -step), lanes(value, step))


def loop(first, last, body, unroll=2):
    count = last - first
    whole = count // unroll if count > unroll else 0

    def step(trip, carry):
        for inner in range(unroll):
            body(first + trip * unroll + inner)
        return carry

    if whole:
        lax.fori_loop(0, whole, step, 0)
    for index in range(first + whole * unroll, last):
        body(index)


def bit(number, height):
    return (lane_index(height) & number) != 0


def place_in_group(level, height):
    return lane_index(height) & (2**level - 1)


def next_x(level, here, after):
    if level == 0:
        return after
    size = 2**level
    last = place_in_group(level, here.shape[0]) == size - 1
    return jnp.where(last, lanes(after, size - 1), lanes(here, -1))


def previous_x(level, here, before):
    if level == 0:
        return before
    size = 2**level
    first = place_in_group(level, here.shape[0]) == 0
    return jnp.where(first, lanes(before, 1 - size), lanes(here, 1))


def pair(level, left, right):
    return (2.0 * 0.25**level) * left * right / (left + right)


def build(level, planes, wrap, b, cx, cxm, cy, cz, czm, diag, gain, f=None, u=None):
    at, height = BUILD[level]
    span, below, above = pl.ds(at, height), pl.ds(at - 1, height), pl.ds(at - 1, height + 8)
    step = 2**level
    lane = lane_index(height)
    top = lane >= 128 - step
    ends = top | (lane < step)

    def along_y(x):
        cy[x, above] = pair(level, b[x, above], b[x, pl.ds(at, height + 8)])

    def one(x, carry):
        c_before, here = carry
        after = b[wrap(x + 1), span]
        c_x = pair(level, here, next_x(level, here, after))
        c_m = previous_x(level, c_x, c_before)
        c_z = jnp.where(top, 0.0, pair(level, here, lanes(here, -step)))
        c_zm = lanes(c_z, step)
        total = c_m + c_x + cy[x, span] + cy[x, below] + c_z + c_zm
        total = total + jnp.where(ends, (0.25**level) * here, 0.0)
        scaled = OMEGA / total
        cx[x, span] = c_x
        if level > 0:
            cxm[x, span] = c_m
            czm[x, span] = c_zm
        cz[x, span] = c_z
        diag[x, span] = total
        gain[x, span] = scaled
        if f is not None:
            u[x, span] = scaled * f[x, span]
        if not (isinstance(x, int) and x == planes[-1]):
            along_y(wrap(x + 1))
        return (c_x, after)

    first = planes[0]
    previous = wrap(first - 1)
    start = b[previous, span]
    before = pair(level, start, next_x(level, start, b[first, span]))
    if level == 0:
        cx[previous, span] = before
    along_y(first)
    carry = (before, b[first, span])
    if len(planes) < 16:
        for x in planes:
            carry = one(x, carry)
        return

    def two(trip, carry):
        carry = one(first + 2 * trip, carry)
        return one(first + 1 + 2 * trip, carry)

    lax.fori_loop(0, len(planes) // 2, two, carry)


def first_sweep(level, planes, u, f, gain):
    span = pl.ds(*BUILD[level])
    for x in planes:
        u[x, span] = gain[x, span] * f[x, span]


def gather(x, u, cx, cxm, cy, cz, czm, at, height):
    span, below = pl.ds(at, height), pl.ds(at - 1, height)
    here = u[x, span]
    along_z = cz[x, span]
    total = cx[x, span] * u[x + 1, span] + cx[x - 1, span] * u[x - 1, span]
    total = total + (cy[x, span] * u[x, pl.ds(at + 1, height)] + cy[x, below] * u[x, below])
    total = total + (along_z * lanes(here, -1) + lanes(along_z * here, 1))
    return here, total


def sweep(first, last, source, target, f, coefs, gain, unroll=4):
    at, height = SPAN[0]
    span = pl.ds(at, height)

    def one(x):
        here, total = gather(x, source, *coefs, at, height)
        target[x, span] = (1.0 - OMEGA) * here + gain[x, span] * (f[x, span] + total)

    loop(first, last, one, unroll)


def packed(level, wrap, u, cx, cxm, cy, cz, czm, at, height):
    span, below = pl.ds(at, height), pl.ds(at - 1, height)
    step = 2**level
    place = place_in_group(level, height)
    is_first, is_last = place == 0, place == step - 1
    kept = {}

    def shifted(x, by):
        if (x, by) not in kept:
            kept[x, by] = lanes(u[x, span], by)
        return kept[x, by]

    def at_plane(x):
        here = u[x, span]
        upper, lower = shifted(x, -step), shifted(x, step)
        after = lanes(jnp.where(is_first, shifted(wrap(x + 1), step), here), -1)
        before = lanes(jnp.where(is_last, shifted(wrap(x - 1), -step), here), 1)
        total = cx[x, span] * after + cxm[x, span] * before
        total = total + (cy[x, span] * u[x, pl.ds(at + 1, height)] + cy[x, below] * u[x, below])
        total = total + (cz[x, span] * upper + czm[x, span] * lower)
        return here, total

    return at_plane


def sweep_packed(level, planes, wrap, source, target, f, coefs, gain, rows_at=None):
    at, height = SPAN[level] if rows_at is None else rows_at
    span = pl.ds(at, height)
    at_plane = packed(level, wrap, source, *coefs, at, height)
    for x in planes:
        here, total = at_plane(x)
        target[x, span] = (1.0 - OMEGA) * here + gain[x, span] * (f[x, span] + total)


def coarsen(level, values):
    height = values[0].shape[0]
    if level == 0:
        even = ~bit(1, height)
        left, right = values[0] + values[1], values[2] + values[3]
        return jnp.where(even, left, right) + jnp.where(even, lanes(left, -1), lanes(right, 1))
    size = 2**level
    sums = []
    for value in values:
        value = value + swap_lanes(value, 1)
        value = value + swap_lanes(value, size)
        if level == 2:
            value = jnp.where(bit(2, height) == bit(1, height), value, swap_lanes(value, 2))
        sums.append(value)
    low, high = (1, 2) if level == 1 else (2, 4)
    lower = jnp.where(bit(low, height), sums[1], sums[0])
    upper = jnp.where(bit(low, height), sums[3], sums[2])
    return jnp.where(bit(high, height), upper, lower)


def refine(level, value):
    height = value.shape[0]
    if level == 0:
        other = swap_lanes(value, 1)
        low = jnp.where(bit(1, height), other, value)
        high = jnp.where(bit(1, height), value, other)
        return [low, low, high, high]
    outer, inner = (2, 1) if level == 1 else (4, 2)
    other = swap_lanes(value, outer)
    result = []
    for half in (jnp.where(bit(outer, height), other, value), jnp.where(bit(outer, height), value, other)):
        swapped = swap_lanes(half, inner)
        result.append(jnp.where(bit(inner, height), swapped, half))
        result.append(jnp.where(bit(inner, height), half, swapped))
    if level == 2:
        same = bit(2, height) == bit(1, height)
        result = [jnp.where(same, part, swap_lanes(part, 1)) for part in result]
    return result


def pair_rows(tmp, slot, value):
    count = value.shape[0] // 2
    tmp[slot, pl.ds(0, 2 * count)] = value
    return tmp[slot, pl.ds(0, count, stride=2)] + tmp[slot, pl.ds(1, count, stride=2)]


def double_rows(tmp, slot, value):
    count = value.shape[0]
    tmp[slot, pl.ds(0, count, stride=2)] = value
    tmp[slot, pl.ds(1, count, stride=2)] = value
    return tmp[slot, pl.ds(0, 2 * count)]


def restrict(level, plane, target, tmp, fine_x, planes, count, at_x, at_row, limit=None):
    def one(i):
        parts = [fine_x + 4 * i + m for m in range(4)]
        if level == 0:
            summed = pair_rows(tmp, i, coarsen(level, [plane(part) for part in parts]))
        else:
            values = []
            for m, part in enumerate(parts):
                part = part if limit is None else min(part, limit)
                values.append(pair_rows(tmp, (4 * i + m) % 20, plane(part)))
            summed = coarsen(level, values)
        target[at_x + i, pl.ds(at_row, count)] = 0.125 * summed

    if level == 0:
        loop(0, planes, one, 2)
    else:
        for i in range(planes):
            one(i)


def field_plane(b, fine_row, count):
    return lambda x: b[x, pl.ds(fine_row, 2 * count)]


def residual_plane(u, f, coefs, diag, fine_row, count):
    def left(x):
        here, total = gather(x, u, *coefs, fine_row, 2 * count)
        span = pl.ds(fine_row, 2 * count)
        return f[x, span] + total - diag[x, span] * here

    return left


def residual_packed(level, wrap, u, f, coefs, diag, fine_row, count):
    at_plane = packed(level, wrap, u, *coefs, fine_row, 2 * count)
    span = pl.ds(fine_row, 2 * count)

    def left(x):
        here, total = at_plane(x)
        return f[x, span] + total - diag[x, span] * here

    return left


def add_coarse(level, u, coarse, tmp, first, last, fine_x, coarse_row, fine_row, count, keep=None):
    span = pl.ds(fine_row, 2 * count)

    def one(i):
        trip = i - first
        parts = refine(level, coarse[i, pl.ds(coarse_row, count)])
        if level == 0:
            low, high = double_rows(tmp, 2 * trip, parts[0]), double_rows(tmp, 2 * trip + 1, parts[2])
            parts = [low, low, high, high]
        for m, part in enumerate(parts):
            x = fine_x + 4 * trip + m
            if keep is None or x in keep:
                if level > 0:
                    part = double_rows(tmp, (4 * trip + m) % 20, part)
                u[x, span] = u[x, span] + part

    if level == 0:
        loop(first, last, one, 2)
    else:
        for i in range(first, last):
            one(i)


def side(offset, length, width, at):
    if offset == 0:
        return pl.ds(0, length), pl.ds(at, length)
    if offset == 1:
        return pl.ds(length - width, width), pl.ds(at - width, width)
    return pl.ds(0, width), pl.ds(at + length, width)


def kernel(nx, ny, f_in, b_in, out, *refs):
    fields = [refs[11 * level : 11 * level + 11] for level in range(4)]
    tmp, load_sem, send_sem, recv_sem, send_2_sem, recv_2_sem, bulk = refs[44:]
    (b0, f0, u0, v0), (b1, f1, u1, v1), (b2, f2, u2, v2), (b3, f3, u3, v3) = [level[:4] for level in fields]
    c0, c1, c2, c3 = [level[4:9] for level in fields]
    (d0, g0), (d1, g1), (d2, g2), (d3, g3) = [level[9:] for level in fields]
    y0, y1, y2, y3 = AT
    mx, my = lax.axis_index("gx"), lax.axis_index("gy")
    far = [(dx, dy) for dx in far_offsets(nx) for dy in (-2, -1, 0, 1, 2) if (dx, dy) != (0, 0)]

    def peer(dx, dy):
        return (lax.rem(mx + dx + nx, nx), lax.rem(my + dy + ny, ny))

    barrier = pltpu.get_barrier_semaphore()
    for dx, dy in NEAR:
        pl.semaphore_signal(barrier, inc=1, device_id=peer(dx, dy), device_id_type=MESH)

    inside = (pl.ds(5, OWN), pl.ds(y0, OWN))
    load_b = pltpu.make_async_copy(b_in, b0.at[inside], load_sem.at[0])
    load_f = pltpu.make_async_copy(f_in, f0.at[inside], load_sem.at[1])
    load_b.start()
    load_f.start()
    pl.semaphore_wait(barrier, len(NEAR))

    started = []

    def send(source, target, dx, dy):
        number = len(started)
        copy = pltpu.make_async_remote_copy(
            src_ref=source,
            dst_ref=target,
            send_sem=send_sem.at[number],
            recv_sem=recv_sem.at[number],
            device_id=peer(dx, dy),
            device_id_type=MESH,
        )
        copy.start()
        started.append(copy)
        return copy

    def send_0(dx, dy, wide, skip=0):
        copies = []
        for source, target, width in ((b_in, b0, wide), (f_in, f0, wide - 1)):
            from_x, to_x = side(dx, OWN, width, 5)
            if skip:
                count = 1
                if dx == 1:
                    from_x, to_x = pl.ds(from_x.start, count), pl.ds(to_x.start, count)
                else:
                    from_x = pl.ds(width - 1, count)
                    to_x = pl.ds(5 + OWN + width - 1, count)
            from_y, to_y = side(dy, OWN, width, y0)
            copies.append(send(source.at[from_x, from_y], target.at[to_x, to_y], dx, dy))
        return copies

    def arrive(copies):
        for copy in copies:
            copy.wait_recv()

    along_y = send_0(0, 1, 5) + send_0(0, -1, 5)
    along_x = send_0(1, 0, 4) + send_0(-1, 0, 4)
    for dx in (1, -1):
        for dy in (1, -1):
            along_x += send_0(dx, dy, 4)

    def send_1(field):
        copies = []
        for dx, dy in NEAR:
            from_x, to_x = side(dx, 8, 3, 4)
            from_y, to_y = side(dy, 16, 6, y1)
            from_x = pl.ds(from_x.start + 4, from_x.size)
            from_y = pl.ds(from_y.start + y1, from_y.size)
            copies.append(send(field.at[from_x, from_y], field.at[to_x, to_y], dx, dy))
        return copies

    def block_2(field, dx, dy):
        return field.at[pl.ds(5 + 2 * dx, 2), pl.ds(y2 + 8 * dy, 8)]

    def send_2(field, number, corners):
        count = 0
        for dx, dy in far:
            if corners or abs(dx) + abs(dy) < 4:
                pltpu.make_async_remote_copy(
                    src_ref=block_2(field, 0, 0),
                    dst_ref=block_2(field, -dx, -dy),
                    send_sem=send_2_sem.at[number],
                    recv_sem=recv_2_sem.at[number],
                    device_id=peer(dx, dy),
                    device_id_type=MESH,
                ).start()
                count += 1
        return bulk.at[pl.ds(0, 2 * count)]

    def wait_2(whole, sems, number):
        pltpu.make_async_copy(whole, whole, sems.at[number]).wait()

    def sent(copies):
        for copy in copies:
            copy.wait_send()

    same = lambda x: x
    ring = nx == 4
    wrap_2 = (lambda x: (x - 1) % 8 + 1) if ring else same
    wrap_3 = (lambda x: (x - 1) % 2 + 1) if ring else same
    planes_1 = range(1, 15)
    inner_1 = range(2, 14)
    planes_2 = range(1, 9) if ring else range(1, 11)
    planes_3 = range(1, 3) if ring else range(1, 4)
    limit = 8 if ring else 10

    load_b.wait()
    restrict(0, field_plane(b0, y0, 16), b1, tmp, 5, 8, 16, 4, y1)
    restrict(1, field_plane(b1, y1, 8), b2, tmp, 4, 2, 8, 5, y2)
    load_f.wait()
    arrive(along_y)
    build(0, range(6, 36), same, b0, *c0, d0, g0, f0, u0)
    sweep(7, 35, u0, v0, f0, c0, g0)
    arrive(along_x)
    middle_b = send_1(b1)
    outer = []
    for dx in (1, -1):
        outer += send_0(dx, 0, 5, 1)
    whole_b = send_2(b2, 0, True)
    build(0, range(2, 6), same, b0, *c0, d0, g0, f0, u0)
    build(0, range(36, 40), same, b0, *c0, d0, g0, f0, u0)
    sweep(3, 7, u0, v0, f0, c0, g0)
    sweep(35, 39, u0, v0, f0, c0, g0)
    sweep(4, 38, v0, u0, f0, c0, g0)
    restrict(0, residual_plane(u0, f0, c0, d0, y0, 16), f1, tmp, 5, 8, 16, 4, y1)
    middle_f = send_1(f1)
    arrive(middle_b)
    build(1, planes_1, same, b1, *c1, d1, g1)
    arrive(outer)
    build(0, range(1, 2), same, b0, *c0, d0, g0, f0, u0)
    build(0, range(40, 41), same, b0, *c0, d0, g0, f0, u0)
    for x in (2, 39):
        sweep(x, x + 1, u0, v0, f0, c0, g0)
    for x in (3, 38):
        sweep(x, x + 1, v0, u0, f0, c0, g0)
    sent(along_y + along_x + middle_b + outer)
    arrive(middle_f)

    first_sweep(1, planes_1, u1, f1, g1)
    sweep_packed(1, inner_1, same, u1, v1, f1, c1, g1)
    sweep_packed(1, inner_1, same, v1, u1, f1, c1, g1)
    restrict(1, residual_packed(1, same, u1, f1, c1, d1, y1, 8), f2, tmp, 4, 2, 8, 5, y2)
    whole_f = send_2(f2, 1, False)
    wait_2(whole_b, recv_2_sem, 0)
    restrict(2, field_plane(b2, 0, 20), b3, tmp, 1, len(planes_3), 20, 1, 0, limit)
    build(2, planes_2, wrap_2, b2, *c2, d2, g2)
    build(3, planes_3, wrap_3, b3, *c3, d3, g3)
    sent(middle_f)
    wait_2(whole_b, send_2_sem, 0)
    wait_2(whole_f, recv_2_sem, 1)

    first_sweep(2, planes_2, u2, f2, g2)
    sweep_packed(2, planes_2, wrap_2, u2, v2, f2, c2, g2)
    sweep_packed(2, planes_2, wrap_2, v2, u2, f2, c2, g2)
    restrict(
        2, residual_packed(2, wrap_2, u2, f2, c2, d2, 4, 16), f3, tmp, 1, len(planes_3), 16, 1, 2, limit
    )

    first_sweep(3, planes_3, u3, f3, g3)
    for _ in range(2):
        sweep_packed(3, planes_3, wrap_3, u3, v3, f3, c3, g3)
        sweep_packed(3, planes_3, wrap_3, v3, u3, f3, c3, g3)

    add_coarse(2, u2, u3, tmp, 1, 3, 1, y3 - 2, y2 - 4, 8, (4, 5, 6, 7))
    middle = (y2 - 4, 16)
    sweep_packed(2, range(4, 8), same, u2, v2, f2, c2, g2, middle)
    sweep_packed(2, range(4, 8), same, v2, u2, f2, c2, g2, middle)

    add_coarse(1, u1, u2, tmp, 4, 8, 0, y2 - 2, y1 - 4, 12, inner_1)
    sweep_packed(1, range(3, 13), same, u1, v1, f1, c1, g1)
    sweep_packed(1, range(3, 13), same, v1, u1, f1, c1, g1)

    add_coarse(0, u0, u1, tmp, 3, 13, 1, y1 - 2, 1, 20)
    sweep(4, 38, u0, v0, f0, c0, g0)

    own = pl.ds(y0, OWN)

    def last(x):
        here, total = gather(x, v0, *c0, y0, OWN)
        out[x - 5] = (1.0 - OMEGA) * here + g0[x, own] * (f0[x, own] + total)

    loop(5, 37, last, 4)
    wait_2(whole_f, send_2_sem, 1)


def solution(mesh):
    nx, ny = mesh.shape["gx"], mesh.shape["gy"]
    copies = 20 + 2 * len(NEAR)
    shapes = []
    for planes, height in zip(PLANES, ROWS):
        shapes += [pltpu.VMEM((planes, height + 8, 128), F32)] + [pltpu.VMEM((planes, height, 128), F32)] * 10

    def per_device(source, inverse_density):
        return pl.pallas_call(
            functools.partial(kernel, nx, ny),
            out_shape=jax.ShapeDtypeStruct(source.shape, F32),
            in_specs=[pl.BlockSpec(memory_space=pl.ANY)] * 2,
            out_specs=pl.BlockSpec(memory_space=pltpu.VMEM),
            scratch_shapes=shapes
            + [
                pltpu.VMEM((20, 48, 128), F32),
                pltpu.SemaphoreType.DMA((2,)),
                pltpu.SemaphoreType.DMA((copies,)),
                pltpu.SemaphoreType.DMA((copies,)),
                pltpu.SemaphoreType.DMA((2,)),
                pltpu.SemaphoreType.DMA((2,)),
                pltpu.VMEM((48, 8, 128), F32),
            ],
            compiler_params=pltpu.CompilerParams(collective_id=0, has_side_effects=True),
        )(source, inverse_density)

    placed = (P("gx", "gy", None), P("gx", "gy", None))
    return jax.shard_map(
        per_device, mesh=mesh, in_specs=placed, out_specs=P("gx", "gy", None), check_vma=False
    )
```

```python
import functools
import math

import jax
import jax.numpy as jnp
from jax import lax
from jax.experimental import pallas as pl
from jax.experimental.pallas import tpu as pltpu
from jax.sharding import PartitionSpec as P

MESH = pl.DeviceIdType.MESH
OMEGA = 0.8
F32 = jnp.float32

PLANES = (42, 16, 12, 5)
ROWS = (48, 40, 48, 32)
AT = (5, 6, 16, 8)
SPAN = ((1, 40), (2, 24), (1, 40), (2, 16))
BUILD = ((1, 40), (1, 32), (1, 40), (2, 16))
OWN = 32
X_0, Y_0, OUTER, B_1, F_1, B_2, F_2 = range(7)
NEAR = [(dx, dy) for dx in (1, -1, 0) for dy in (0, 1, -1) if (dx, dy) != (0, 0)]


def far_offsets(peers):
    return (-1, 0, 1, 2) if peers == 4 else (-2, -1, 0, 1, 2)


def lanes(value, shift):
    return pltpu.roll(value, shift % 128, 1)


def rows(value, shift):
    return pltpu.roll(value, shift % value.shape[0], 0)


def lane_index(height):
    return lax.broadcasted_iota(jnp.int32, (height, 128), 1)


def swap_lanes(value, step):
    low = (lane_index(value.shape[0]) & step) == 0
    return jnp.where(low, lanes(value, -step), lanes(value, step))


def loop(first, last, body, unroll=2):
    count = last - first
    whole = count // unroll if count > unroll else 0

    def step(trip, carry):
        for inner in range(unroll):
            body(first + trip * unroll + inner)
        return carry

    if whole:
        lax.fori_loop(0, whole, step, 0)
    for index in range(first + whole * unroll, last):
        body(index)


def bit(number, height):
    return (lane_index(height) & number) != 0


def place_in_group(level, height):
    return lane_index(height) & (2**level - 1)


def next_x(level, here, after):
    if level == 0:
        return after
    size = 2**level
    last = place_in_group(level, here.shape[0]) == size - 1
    return jnp.where(last, lanes(after, size - 1), lanes(here, -1))


def previous_x(level, here, before):
    if level == 0:
        return before
    size = 2**level
    first = place_in_group(level, here.shape[0]) == 0
    return jnp.where(first, lanes(before, 1 - size), lanes(here, 1))


def pair(level, left, right):
    return (2.0 * 0.25**level) * left * right / (left + right)


def build(level, planes, wrap, b, cx, cxm, cy, cz, czm, diag, gain, f=None, u=None, rows=None, faces=None):
    at, height = BUILD[level] if rows is None else rows
    span, below = pl.ds(at, height), pl.ds(at - 1, height)
    low, faces = (at - 1, height + 8) if faces is None else faces
    step = 2**level
    lane = lane_index(height)
    top = lane >= 128 - step
    ends = top | (lane < step)

    def along_y(x):
        lower = pl.ds(low, faces)
        cy[x, lower] = pair(level, b[x, lower], b[x, pl.ds(low + 1, faces)])

    def one(x, carry):
        c_before, here = carry
        after = b[wrap(x + 1), span]
        c_x = pair(level, here, next_x(level, here, after))
        c_m = previous_x(level, c_x, c_before)
        c_z = jnp.where(top, 0.0, pair(level, here, lanes(here, -step)))
        c_zm = lanes(c_z, step)
        total = c_m + c_x + cy[x, span] + cy[x, below] + c_z + c_zm
        total = total + jnp.where(ends, (0.25**level) * here, 0.0)
        scaled = OMEGA / total
        cx[x, span] = c_x
        if level > 0:
            cxm[x, span] = c_m
            czm[x, span] = c_zm
        cz[x, span] = c_z
        diag[x, span] = total
        gain[x, span] = scaled
        if f is not None:
            u[x, span] = scaled * f[x, span]
        if not (isinstance(x, int) and x == planes[-1]):
            along_y(wrap(x + 1))
        return (c_x, after)

    first = planes[0]
    previous = wrap(first - 1)
    start = b[previous, span]
    before = pair(level, start, next_x(level, start, b[first, span]))
    if level == 0:
        cx[previous, span] = before
    along_y(first)
    carry = (before, b[first, span])
    if len(planes) < 16:
        for x in planes:
            carry = one(x, carry)
        return

    group = 5 if height > 8 else 15

    def some(trip, carry):
        for inner in range(group):
            carry = one(first + group * trip + inner, carry)
        return carry

    lax.fori_loop(0, len(planes) // group, some, carry)


def first_sweep(level, planes, u, f, gain):
    span = pl.ds(*BUILD[level])
    for x in planes:
        u[x, span] = gain[x, span] * f[x, span]


def gather(x, u, cx, cxm, cy, cz, czm, at, height):
    span, below = pl.ds(at, height), pl.ds(at - 1, height)
    here = u[x, span]
    along_z = cz[x, span]
    total = cx[x, span] * u[x + 1, span] + cx[x - 1, span] * u[x - 1, span]
    total = total + (cy[x, span] * u[x, pl.ds(at + 1, height)] + cy[x, below] * u[x, below])
    total = total + (along_z * lanes(here, -1) + lanes(along_z * here, 1))
    return here, total


def sweep(first, last, source, target, f, coefs, gain, rows=SPAN[0], unroll=None):
    at, height = rows
    unroll = (84 if height > 8 else 112) // (-(-height // 8)) if unroll is None else unroll
    span = pl.ds(at, height)

    def one(x):
        here, total = gather(x, source, *coefs, at, height)
        target[x, span] = (1.0 - OMEGA) * here + gain[x, span] * (f[x, span] + total)

    loop(first, last, one, unroll)


def packed(level, wrap, u, cx, cxm, cy, cz, czm, at, height):
    span, below = pl.ds(at, height), pl.ds(at - 1, height)
    step = 2**level
    place = place_in_group(level, height)
    is_first, is_last = place == 0, place == step - 1
    kept = {}

    def shifted(x, by):
        if (x, by) not in kept:
            kept[x, by] = lanes(u[x, span], by)
        return kept[x, by]

    def at_plane(x):
        here = u[x, span]
        upper, lower = shifted(x, -step), shifted(x, step)
        after = lanes(jnp.where(is_first, shifted(wrap(x + 1), step), here), -1)
        before = lanes(jnp.where(is_last, shifted(wrap(x - 1), -step), here), 1)
        total = cx[x, span] * after + cxm[x, span] * before
        total = total + (cy[x, span] * u[x, pl.ds(at + 1, height)] + cy[x, below] * u[x, below])
        total = total + (cz[x, span] * upper + czm[x, span] * lower)
        return here, total

    return at_plane


def sweep_packed(level, planes, wrap, source, target, f, coefs, gain, rows_at=None):
    at, height = SPAN[level] if rows_at is None else rows_at
    span = pl.ds(at, height)
    at_plane = packed(level, wrap, source, *coefs, at, height)
    for x in planes:
        here, total = at_plane(x)
        target[x, span] = (1.0 - OMEGA) * here + gain[x, span] * (f[x, span] + total)


def coarsen(level, values):
    height = values[0].shape[0]
    if level == 0:
        even = ~bit(1, height)
        left, right = values[0] + values[1], values[2] + values[3]
        return jnp.where(even, left, right) + jnp.where(even, lanes(left, -1), lanes(right, 1))
    size = 2**level
    sums = []
    for value in values:
        value = value + swap_lanes(value, 1)
        value = value + swap_lanes(value, size)
        if level == 2:
            value = jnp.where(bit(2, height) == bit(1, height), value, swap_lanes(value, 2))
        sums.append(value)
    low, high = (1, 2) if level == 1 else (2, 4)
    lower = jnp.where(bit(low, height), sums[1], sums[0])
    upper = jnp.where(bit(low, height), sums[3], sums[2])
    return jnp.where(bit(high, height), upper, lower)


def refine(level, value):
    height = value.shape[0]
    if level == 0:
        other = swap_lanes(value, 1)
        low = jnp.where(bit(1, height), other, value)
        high = jnp.where(bit(1, height), value, other)
        return [low, low, high, high]
    outer, inner = (2, 1) if level == 1 else (4, 2)
    other = swap_lanes(value, outer)
    result = []
    for half in (jnp.where(bit(outer, height), other, value), jnp.where(bit(outer, height), value, other)):
        swapped = swap_lanes(half, inner)
        result.append(jnp.where(bit(inner, height), swapped, half))
        result.append(jnp.where(bit(inner, height), half, swapped))
    if level == 2:
        same = bit(2, height) == bit(1, height)
        result = [jnp.where(same, part, swap_lanes(part, 1)) for part in result]
    return result


def pair_rows(tmp, slot, value):
    count = value.shape[0] // 2
    tmp[slot, pl.ds(0, 2 * count)] = value
    return tmp[slot, pl.ds(0, count, stride=2)] + tmp[slot, pl.ds(1, count, stride=2)]


def double_rows(tmp, slot, value):
    count = value.shape[0]
    tmp[slot, pl.ds(0, count, stride=2)] = value
    tmp[slot, pl.ds(1, count, stride=2)] = value
    return tmp[slot, pl.ds(0, 2 * count)]


def restrict(level, plane, target, tmp, fine_x, planes, count, at_x, at_row, limit=None):
    def one(i):
        parts = [fine_x + 4 * i + m for m in range(4)]
        if level == 0:
            summed = pair_rows(tmp, i, coarsen(level, [plane(part) for part in parts]))
        else:
            values = []
            for m, part in enumerate(parts):
                part = part if limit is None else min(part, limit)
                values.append(pair_rows(tmp, (4 * i + m) % 20, plane(part)))
            summed = coarsen(level, values)
        target[at_x + i, pl.ds(at_row, count)] = 0.125 * summed

    if level == 0:
        loop(0, planes, one, 2)
    else:
        for i in range(planes):
            one(i)


def field_plane(b, fine_row, count):
    return lambda x: b[x, pl.ds(fine_row, 2 * count)]


def residual_plane(u, f, coefs, diag, fine_row, count):
    def left(x):
        here, total = gather(x, u, *coefs, fine_row, 2 * count)
        span = pl.ds(fine_row, 2 * count)
        return f[x, span] + total - diag[x, span] * here

    return left


def residual_packed(level, wrap, u, f, coefs, diag, fine_row, count):
    at_plane = packed(level, wrap, u, *coefs, fine_row, 2 * count)
    span = pl.ds(fine_row, 2 * count)

    def left(x):
        here, total = at_plane(x)
        return f[x, span] + total - diag[x, span] * here

    return left


def add_coarse(level, u, coarse, tmp, first, last, fine_x, coarse_row, fine_row, count, keep=None):
    span = pl.ds(fine_row, 2 * count)

    def one(i):
        trip = i - first
        parts = refine(level, coarse[i, pl.ds(coarse_row, count)])
        if level == 0:
            low, high = double_rows(tmp, 2 * trip, parts[0]), double_rows(tmp, 2 * trip + 1, parts[2])
            parts = [low, low, high, high]
        for m, part in enumerate(parts):
            x = fine_x + 4 * trip + m
            if keep is None or x in keep:
                if level > 0:
                    part = double_rows(tmp, (4 * trip + m) % 20, part)
                u[x, span] = u[x, span] + part

    if level == 0:
        loop(first, last, one, 2)
    else:
        for i in range(first, last):
            one(i)


def side(offset, length, width, at):
    if offset == 0:
        return pl.ds(0, length), pl.ds(at, length)
    if offset == 1:
        return pl.ds(length - width, width), pl.ds(at - width, width)
    return pl.ds(0, width), pl.ds(at + length, width)


def kernel(nx, ny, f_in, b_in, out, *refs):
    fields = [refs[11 * level : 11 * level + 11] for level in range(4)]
    tmp, load_sem, send_sem, recv_sem, bulk = refs[44:]
    (b0, f0, u0, v0), (b1, f1, u1, v1), (b2, f2, u2, v2), (b3, f3, u3, v3) = [level[:4] for level in fields]
    c0, c1, c2, c3 = [level[4:9] for level in fields]
    (d0, g0), (d1, g1), (d2, g2), (d3, g3) = [level[9:] for level in fields]
    w0 = c0[4]
    y0, y1, y2, y3 = AT
    mx, my = lax.axis_index("gx"), lax.axis_index("gy")
    far = [(dx, dy) for dx in far_offsets(nx) for dy in (-2, -1, 0, 1, 2) if (dx, dy) != (0, 0)]

    def peer(dx, dy):
        return (lax.rem(mx + dx + nx, nx), lax.rem(my + dy + ny, ny))

    barrier = pltpu.get_barrier_semaphore()
    for dx, dy in NEAR:
        pl.semaphore_signal(barrier, inc=1, device_id=peer(dx, dy), device_id_type=MESH)

    inside = (pl.ds(5, OWN), pl.ds(y0, OWN))
    load_b = pltpu.make_async_copy(b_in, b0.at[inside], load_sem.at[0])
    load_f = pltpu.make_async_copy(f_in, f0.at[inside], load_sem.at[1])
    load_b.start()
    load_f.start()
    load_b.wait()
    restrict(0, field_plane(b0, y0, 16), b1, tmp, 5, 8, 16, 4, y1)
    restrict(1, field_plane(b1, y1, 8), b2, tmp, 4, 2, 8, 5, y2)
    load_f.wait()
    same = lambda x: x
    build(0, range(6, 36), same, b0, *c0, d0, g0, f0, u0, (y0 + 1, OWN - 2), (y0, OWN - 1))
    pl.semaphore_wait(barrier, len(NEAR))

    sizes = {}

    def send(source, target, dx, dy, group):
        copy = pltpu.make_async_remote_copy(
            src_ref=source,
            dst_ref=target,
            send_sem=send_sem.at[0],
            recv_sem=recv_sem.at[group],
            device_id=peer(dx, dy),
            device_id_type=MESH,
        )
        copy.start()
        sizes[group] = sizes.get(group, 0) + math.prod(source.shape[:-1])

    def settle(sems, number, count):
        whole = bulk.at[pl.ds(0, count)]
        pltpu.make_async_copy(whole, whole, sems.at[number]).wait()

    def arrive(group):
        settle(recv_sem, group, sizes[group])

    def send_0(dx, dy, wide, group, skip=0):
        for source, target, width in ((b_in, b0, wide), (f_in, f0, wide - 1)):
            from_x, to_x = side(dx, OWN, width, 5)
            if skip:
                count = 1
                if dx == 1:
                    from_x, to_x = pl.ds(from_x.start, count), pl.ds(to_x.start, count)
                else:
                    from_x = pl.ds(width - 1, count)
                    to_x = pl.ds(5 + OWN + width - 1, count)
            from_y, to_y = side(dy, OWN, width, y0)
            send(source.at[from_x, from_y], target.at[to_x, to_y], dx, dy, group)

    def send_1(field, group):
        for dx, dy in NEAR:
            from_x, to_x = side(dx, 8, 3, 4)
            from_y, to_y = side(dy, 16, 6, y1)
            from_x = pl.ds(from_x.start + 4, from_x.size)
            from_y = pl.ds(from_y.start + y1, from_y.size)
            send(field.at[from_x, from_y], field.at[to_x, to_y], dx, dy, group)

    def block_2(field, dx, dy):
        return field.at[pl.ds(5 + 2 * dx, 2), pl.ds(y2 + 8 * dy, 8)]

    def send_2(field, group, corners):
        for dx, dy in far:
            if corners or abs(dx) + abs(dy) < 4:
                send(block_2(field, 0, 0), block_2(field, -dx, -dy), dx, dy, group)

    ring = nx == 4
    wrap_2 = (lambda x: (x - 1) % 8 + 1) if ring else same
    wrap_3 = (lambda x: (x - 1) % 2 + 1) if ring else same
    planes_1 = range(1, 15)
    inner_1 = range(2, 14)
    planes_2 = range(1, 9) if ring else range(1, 11)
    planes_3 = range(1, 3) if ring else range(1, 4)
    limit = 8 if ring else 10

    send_0(1, 0, 4, X_0)
    send_0(-1, 0, 4, X_0)
    send_0(0, 1, 5, Y_0)
    send_0(0, -1, 5, Y_0)
    for dx in (1, -1):
        for dy in (1, -1):
            send_0(dx, dy, 4, X_0)

    send_1(b1, B_1)
    for dx in (1, -1):
        send_0(dx, 0, 5, OUTER, 1)

    def fold(first, count):
        plane = residual_plane(w0, f0, c0, d0, y0, 16)
        restrict(0, plane, f1, tmp, 5 + 4 * first, count, 16, 4 + first, y1)

    sweep(7, 35, u0, v0, f0, c0, g0, (y0 + 2, OWN - 4))
    sweep(8, 34, v0, w0, f0, c0, g0, (y0 + 3, OWN - 6))
    arrive(Y_0)
    for at in (1, 33):
        build(0, range(6, 36), same, b0, *c0, d0, g0, f0, u0, (at, 8))
    for at in (2, 32):
        sweep(7, 35, u0, v0, f0, c0, g0, (at, 8))
    for at in (3, 31):
        sweep(8, 34, v0, w0, f0, c0, g0, (at, 8))
    fold(1, 6)
    arrive(X_0)
    build(0, range(2, 6), same, b0, *c0, d0, g0, f0, u0)
    build(0, range(36, 40), same, b0, *c0, d0, g0, f0, u0)
    sweep(3, 7, u0, v0, f0, c0, g0)
    sweep(35, 39, u0, v0, f0, c0, g0)
    sweep(4, 8, v0, w0, f0, c0, g0)
    sweep(34, 38, v0, w0, f0, c0, g0)
    fold(0, 1)
    fold(7, 1)
    send_1(f1, F_1)
    send_2(b2, B_2, True)
    arrive(B_1)
    build(1, planes_1, same, b1, *c1, d1, g1)
    arrive(OUTER)
    build(0, range(1, 2), same, b0, *c0, d0, g0, f0, u0)
    build(0, range(40, 41), same, b0, *c0, d0, g0, f0, u0)
    for x in (2, 39):
        sweep(x, x + 1, u0, v0, f0, c0, g0)
    for x in (3, 38):
        sweep(x, x + 1, v0, w0, f0, c0, g0)
    arrive(F_1)

    first_sweep(1, planes_1, u1, f1, g1)
    sweep_packed(1, inner_1, same, u1, v1, f1, c1, g1)
    sweep_packed(1, inner_1, same, v1, u1, f1, c1, g1)
    restrict(1, residual_packed(1, same, u1, f1, c1, d1, y1, 8), f2, tmp, 4, 2, 8, 5, y2)
    send_2(f2, F_2, False)
    arrive(B_2)
    restrict(2, field_plane(b2, 0, 20), b3, tmp, 1, len(planes_3), 20, 1, 0, limit)
    build(2, planes_2, wrap_2, b2, *c2, d2, g2)
    build(3, planes_3, wrap_3, b3, *c3, d3, g3)
    arrive(F_2)

    first_sweep(2, planes_2, u2, f2, g2)
    sweep_packed(2, planes_2, wrap_2, u2, v2, f2, c2, g2)
    sweep_packed(2, planes_2, wrap_2, v2, u2, f2, c2, g2)
    restrict(
        2, residual_packed(2, wrap_2, u2, f2, c2, d2, 4, 16), f3, tmp, 1, len(planes_3), 16, 1, 2, limit
    )

    first_sweep(3, planes_3, u3, f3, g3)
    for _ in range(2):
        sweep_packed(3, planes_3, wrap_3, u3, v3, f3, c3, g3)
        sweep_packed(3, planes_3, wrap_3, v3, u3, f3, c3, g3)

    add_coarse(2, u2, u3, tmp, 1, 3, 1, y3 - 2, y2 - 4, 8, (4, 5, 6, 7))
    middle = (y2 - 4, 16)
    sweep_packed(2, range(4, 8), same, u2, v2, f2, c2, g2, middle)
    sweep_packed(2, range(4, 8), same, v2, u2, f2, c2, g2, middle)

    add_coarse(1, u1, u2, tmp, 4, 8, 0, y2 - 2, y1 - 4, 12, inner_1)
    sweep_packed(1, range(3, 13), same, u1, v1, f1, c1, g1)
    sweep_packed(1, range(3, 13), same, v1, u1, f1, c1, g1)

    add_coarse(0, w0, u1, tmp, 3, 13, 1, y1 - 2, 1, 20)
    sweep(4, 38, w0, v0, f0, c0, g0)

    own = pl.ds(y0, OWN)

    def last(x):
        here, total = gather(x, v0, *c0, y0, OWN)
        out[x - 5] = (1.0 - OMEGA) * here + g0[x, own] * (f0[x, own] + total)

    loop(5, 37, last, 16)
    settle(send_sem, 0, sum(sizes.values()))


def solution(mesh):
    nx, ny = mesh.shape["gx"], mesh.shape["gy"]
    shapes = []
    for planes, height in zip(PLANES, ROWS):
        shapes += [pltpu.VMEM((planes, height + 8, 128), F32)] + [pltpu.VMEM((planes, height, 128), F32)] * 10

    def per_device(source, inverse_density):
        return pl.pallas_call(
            functools.partial(kernel, nx, ny),
            out_shape=jax.ShapeDtypeStruct(source.shape, F32),
            in_specs=[pl.BlockSpec(memory_space=pl.ANY)] * 2,
            out_specs=pl.BlockSpec(memory_space=pltpu.VMEM),
            scratch_shapes=shapes
            + [
                pltpu.VMEM((20, 48, 128), F32),
                pltpu.SemaphoreType.DMA((2,)),
                pltpu.SemaphoreType.DMA((1,)),
                pltpu.SemaphoreType.DMA((7,)),
                pltpu.VMEM((5120, 128), F32),
            ],
            compiler_params=pltpu.CompilerParams(collective_id=0, has_side_effects=True),
        )(source, inverse_density)

    placed = (P("gx", "gy", None), P("gx", "gy", None))
    return jax.shard_map(
        per_device, mesh=mesh, in_specs=placed, out_specs=P("gx", "gy", None), check_vma=False
    )
```

```python
import functools
import math

import jax
import jax.numpy as jnp
from jax import lax
from jax.experimental import pallas as pl
from jax.experimental.pallas import tpu as pltpu
from jax.sharding import PartitionSpec as P

MESH = pl.DeviceIdType.MESH
OMEGA = 0.8
F32 = jnp.float32

PLANES = (42, 16, 12, 5)
ROWS = (48, 40, 48, 32)
AT = (5, 6, 16, 8)
SPAN = ((1, 40), (2, 24), (1, 40), (2, 16))
BUILD = ((1, 40), (1, 32), (1, 40), (2, 16))
OWN = 32
X_0, Y_0, OUTER, B_1, F_1, B_2, F_2 = range(7)
NEAR = [(dx, dy) for dx in (1, -1, 0) for dy in (0, 1, -1) if (dx, dy) != (0, 0)]


def far_offsets(peers):
    return (-1, 0, 1, 2) if peers == 4 else (-2, -1, 0, 1, 2)


def lanes(value, shift):
    return pltpu.roll(value, shift % 128, 1)


def rows(value, shift):
    return pltpu.roll(value, shift % value.shape[0], 0)


def lane_index(height):
    return lax.broadcasted_iota(jnp.int32, (height, 128), 1)


def swap_lanes(value, step):
    low = (lane_index(value.shape[0]) & step) == 0
    return jnp.where(low, lanes(value, -step), lanes(value, step))


def loop(first, last, body, unroll=2):
    count = last - first
    whole = count // unroll if count > unroll else 0

    def step(trip, carry):
        for inner in range(unroll):
            body(first + trip * unroll + inner)
        return carry

    if whole:
        lax.fori_loop(0, whole, step, 0)
    for index in range(first + whole * unroll, last):
        body(index)


def bit(number, height):
    return (lane_index(height) & number) != 0


def place_in_group(level, height):
    return lane_index(height) & (2**level - 1)


def next_x(level, here, after):
    if level == 0:
        return after
    size = 2**level
    last = place_in_group(level, here.shape[0]) == size - 1
    return jnp.where(last, lanes(after, size - 1), lanes(here, -1))


def previous_x(level, here, before):
    if level == 0:
        return before
    size = 2**level
    first = place_in_group(level, here.shape[0]) == 0
    return jnp.where(first, lanes(before, 1 - size), lanes(here, 1))


def pair(level, left, right):
    return (2.0 * 0.25**level) * left * right / (left + right)


def build(level, planes, wrap, b, cx, cxm, cy, cz, czm, diag, gain, f=None, u=None, rows=None, faces=None):
    at, height = BUILD[level] if rows is None else rows
    span, below = pl.ds(at, height), pl.ds(at - 1, height)
    low, faces = (at - 1, height + 8) if faces is None else faces
    step = 2**level
    lane = lane_index(height)
    top = lane >= 128 - step
    ends = top | (lane < step)

    def along_y(x):
        lower = pl.ds(low, faces)
        cy[x, lower] = pair(level, b[x, lower], b[x, pl.ds(low + 1, faces)])

    def one(x, carry):
        c_before, here = carry
        after = b[wrap(x + 1), span]
        c_x = pair(level, here, next_x(level, here, after))
        c_m = previous_x(level, c_x, c_before)
        c_z = jnp.where(top, 0.0, pair(level, here, lanes(here, -step)))
        c_zm = lanes(c_z, step)
        total = c_m + c_x + cy[x, span] + cy[x, below] + c_z + c_zm
        total = total + jnp.where(ends, (0.25**level) * here, 0.0)
        scaled = OMEGA / total
        cx[x, span] = c_x
        if level > 0:
            cxm[x, span] = c_m
            czm[x, span] = c_zm
        cz[x, span] = c_z
        diag[x, span] = total
        gain[x, span] = scaled
        if f is not None:
            u[x, span] = scaled * f[x, span]
        if not (isinstance(x, int) and x == planes[-1]):
            along_y(wrap(x + 1))
        return (c_x, after)

    first = planes[0]
    previous = wrap(first - 1)
    start = b[previous, span]
    before = pair(level, start, next_x(level, start, b[first, span]))
    if level == 0:
        cx[previous, span] = before
    along_y(first)
    carry = (before, b[first, span])
    if len(planes) < 16:
        for x in planes:
            carry = one(x, carry)
        return

    group = 5 if height > 8 else 15

    def some(trip, carry):
        for inner in range(group):
            carry = one(first + group * trip + inner, carry)
        return carry

    lax.fori_loop(0, len(planes) // group, some, carry)


def first_sweep(level, planes, u, f, gain):
    span = pl.ds(*BUILD[level])
    for x in planes:
        u[x, span] = gain[x, span] * f[x, span]


def gather(x, u, cx, cxm, cy, cz, czm, at, height):
    span, below = pl.ds(at, height), pl.ds(at - 1, height)
    here = u[x, span]
    along_z = cz[x, span]
    total = cx[x, span] * u[x + 1, span] + cx[x - 1, span] * u[x - 1, span]
    total = total + (cy[x, span] * u[x, pl.ds(at + 1, height)] + cy[x, below] * u[x, below])
    total = total + (along_z * lanes(here, -1) + lanes(along_z * here, 1))
    return here, total


def sweep(first, last, source, target, f, coefs, gain, rows=SPAN[0], unroll=None):
    at, height = rows
    unroll = (84 if height > 8 else 112) // (-(-height // 8)) if unroll is None else unroll
    span = pl.ds(at, height)

    def one(x):
        here, total = gather(x, source, *coefs, at, height)
        target[x, span] = (1.0 - OMEGA) * here + gain[x, span] * (f[x, span] + total)

    loop(first, last, one, unroll)


def packed(level, wrap, u, cx, cxm, cy, cz, czm, at, height):
    span, below = pl.ds(at, height), pl.ds(at - 1, height)
    step = 2**level
    place = place_in_group(level, height)
    is_first, is_last = place == 0, place == step - 1
    kept = {}

    def shifted(x, by):
        if (x, by) not in kept:
            kept[x, by] = lanes(u[x, span], by)
        return kept[x, by]

    def at_plane(x):
        here = u[x, span]
        upper, lower = shifted(x, -step), shifted(x, step)
        if level == 3:
            after = next_x(level, here, u[wrap(x + 1), span])
            before = previous_x(level, here, u[wrap(x - 1), span])
        else:
            after = lanes(jnp.where(is_first, shifted(wrap(x + 1), step), here), -1)
            before = lanes(jnp.where(is_last, shifted(wrap(x - 1), -step), here), 1)
        total = cx[x, span] * after + cxm[x, span] * before
        total = total + (cy[x, span] * u[x, pl.ds(at + 1, height)] + cy[x, below] * u[x, below])
        total = total + (cz[x, span] * upper + czm[x, span] * lower)
        return here, total

    return at_plane


def sweep_packed(level, planes, wrap, source, target, f, coefs, gain, rows_at=None):
    at, height = SPAN[level] if rows_at is None else rows_at
    span = pl.ds(at, height)
    at_plane = packed(level, wrap, source, *coefs, at, height)
    for x in planes:
        here, total = at_plane(x)
        target[x, span] = (1.0 - OMEGA) * here + gain[x, span] * (f[x, span] + total)


def coarsen(level, values):
    height = values[0].shape[0]
    if level == 0:
        even = ~bit(1, height)
        left, right = values[0] + values[1], values[2] + values[3]
        return jnp.where(even, left, right) + jnp.where(even, lanes(left, -1), lanes(right, 1))
    size = 2**level
    sums = []
    for value in values:
        value = value + swap_lanes(value, 1)
        value = value + swap_lanes(value, size)
        if level == 2:
            value = jnp.where(bit(2, height) == bit(1, height), value, swap_lanes(value, 2))
        sums.append(value)
    low, high = (1, 2) if level == 1 else (2, 4)
    lower = jnp.where(bit(low, height), sums[1], sums[0])
    upper = jnp.where(bit(low, height), sums[3], sums[2])
    return jnp.where(bit(high, height), upper, lower)


def refine(level, value):
    height = value.shape[0]
    if level == 0:
        other = swap_lanes(value, 1)
        low = jnp.where(bit(1, height), other, value)
        high = jnp.where(bit(1, height), value, other)
        return [low, low, high, high]
    outer, inner = (2, 1) if level == 1 else (4, 2)
    other = swap_lanes(value, outer)
    result = []
    for half in (jnp.where(bit(outer, height), other, value), jnp.where(bit(outer, height), value, other)):
        swapped = swap_lanes(half, inner)
        result.append(jnp.where(bit(inner, height), swapped, half))
        result.append(jnp.where(bit(inner, height), half, swapped))
    if level == 2:
        same = bit(2, height) == bit(1, height)
        result = [jnp.where(same, part, swap_lanes(part, 1)) for part in result]
    return result


def pair_rows(tmp, slot, value):
    count = value.shape[0] // 2
    tmp[slot, pl.ds(0, 2 * count)] = value
    return tmp[slot, pl.ds(0, count, stride=2)] + tmp[slot, pl.ds(1, count, stride=2)]


def double_rows(tmp, slot, value):
    count = value.shape[0]
    tmp[slot, pl.ds(0, count, stride=2)] = value
    tmp[slot, pl.ds(1, count, stride=2)] = value
    return tmp[slot, pl.ds(0, 2 * count)]


def restrict(level, plane, target, tmp, fine_x, planes, count, at_x, at_row, limit=None):
    def one(i):
        parts = [fine_x + 4 * i + m for m in range(4)]
        if level == 0:
            summed = pair_rows(tmp, i, coarsen(level, [plane(part) for part in parts]))
        else:
            values = []
            for m, part in enumerate(parts):
                part = part if limit is None else min(part, limit)
                values.append(pair_rows(tmp, (4 * i + m) % 20, plane(part)))
            summed = coarsen(level, values)
        target[at_x + i, pl.ds(at_row, count)] = 0.125 * summed

    if level == 0:
        loop(0, planes, one, 2)
    else:
        for i in range(planes):
            one(i)


def field_plane(b, fine_row, count):
    return lambda x: b[x, pl.ds(fine_row, 2 * count)]


def residual_plane(u, f, coefs, diag, fine_row, count):
    def left(x):
        here, total = gather(x, u, *coefs, fine_row, 2 * count)
        span = pl.ds(fine_row, 2 * count)
        return f[x, span] + total - diag[x, span] * here

    return left


def residual_packed(level, wrap, u, f, coefs, diag, fine_row, count):
    at_plane = packed(level, wrap, u, *coefs, fine_row, 2 * count)
    span = pl.ds(fine_row, 2 * count)

    def left(x):
        here, total = at_plane(x)
        return f[x, span] + total - diag[x, span] * here

    return left


def add_coarse(level, u, coarse, tmp, first, last, fine_x, coarse_row, fine_row, count, keep=None):
    span = pl.ds(fine_row, 2 * count)

    def one(i):
        trip = i - first
        parts = refine(level, coarse[i, pl.ds(coarse_row, count)])
        if level == 0:
            low, high = double_rows(tmp, 2 * trip, parts[0]), double_rows(tmp, 2 * trip + 1, parts[2])
            parts = [low, low, high, high]
        for m, part in enumerate(parts):
            x = fine_x + 4 * trip + m
            if keep is None or x in keep:
                if level > 0:
                    part = double_rows(tmp, (4 * trip + m) % 20, part)
                u[x, span] = u[x, span] + part

    if level == 0:
        loop(first, last, one, 2)
    else:
        for i in range(first, last):
            one(i)


def side(offset, length, width, at):
    if offset == 0:
        return pl.ds(0, length), pl.ds(at, length)
    if offset == 1:
        return pl.ds(length - width, width), pl.ds(at - width, width)
    return pl.ds(0, width), pl.ds(at + length, width)


def kernel(nx, ny, f_in, b_in, out, *refs):
    fields = [refs[11 * level : 11 * level + 11] for level in range(4)]
    tmp, load_sem, send_sem, recv_sem, bulk = refs[44:]
    (b0, f0, u0, v0), (b1, f1, u1, v1), (b2, f2, u2, v2), (b3, f3, u3, v3) = [level[:4] for level in fields]
    c0, c1, c2, c3 = [level[4:9] for level in fields]
    (d0, g0), (d1, g1), (d2, g2), (d3, g3) = [level[9:] for level in fields]
    w0 = c0[4]
    y0, y1, y2, y3 = AT
    mx, my = lax.axis_index("gx"), lax.axis_index("gy")
    far = [(dx, dy) for dx in far_offsets(nx) for dy in (-2, -1, 0, 1, 2) if (dx, dy) != (0, 0)]

    def peer(dx, dy):
        return (lax.rem(mx + dx + nx, nx), lax.rem(my + dy + ny, ny))

    barrier = pltpu.get_barrier_semaphore()
    for dx, dy in NEAR:
        pl.semaphore_signal(barrier, inc=1, device_id=peer(dx, dy), device_id_type=MESH)

    inside = (pl.ds(5, OWN), pl.ds(y0, OWN))
    load_b = pltpu.make_async_copy(b_in, b0.at[inside], load_sem.at[0])
    load_f = pltpu.make_async_copy(f_in, f0.at[inside], load_sem.at[1])
    load_b.start()
    load_f.start()
    load_b.wait()
    restrict(0, field_plane(b0, y0, 16), b1, tmp, 5, 8, 16, 4, y1)
    restrict(1, field_plane(b1, y1, 8), b2, tmp, 4, 2, 8, 5, y2)
    load_f.wait()
    same = lambda x: x
    build(0, range(6, 36), same, b0, *c0, d0, g0, f0, u0, (y0 + 1, OWN - 2), (y0, OWN - 1))
    pl.semaphore_wait(barrier, len(NEAR))

    sizes = {}

    def send(source, target, dx, dy, group):
        copy = pltpu.make_async_remote_copy(
            src_ref=source,
            dst_ref=target,
            send_sem=send_sem.at[0],
            recv_sem=recv_sem.at[group],
            device_id=peer(dx, dy),
            device_id_type=MESH,
        )
        copy.start()
        sizes[group] = sizes.get(group, 0) + math.prod(source.shape[:-1])

    def settle(sems, number, count):
        whole = bulk.at[pl.ds(0, count)]
        pltpu.make_async_copy(whole, whole, sems.at[number]).wait()

    def arrive(group):
        settle(recv_sem, group, sizes[group])

    def send_0(dx, dy, wide, group, skip=0):
        for source, target, width in ((b_in, b0, wide), (f_in, f0, wide - 1)):
            from_x, to_x = side(dx, OWN, width, 5)
            if skip:
                count = 1
                if dx == 1:
                    from_x, to_x = pl.ds(from_x.start, count), pl.ds(to_x.start, count)
                else:
                    from_x = pl.ds(width - 1, count)
                    to_x = pl.ds(5 + OWN + width - 1, count)
            from_y, to_y = side(dy, OWN, width, y0)
            send(source.at[from_x, from_y], target.at[to_x, to_y], dx, dy, group)

    def send_1(field, group):
        for dx, dy in NEAR:
            from_x, to_x = side(dx, 8, 3, 4)
            from_y, to_y = side(dy, 16, 6, y1)
            from_x = pl.ds(from_x.start + 4, from_x.size)
            from_y = pl.ds(from_y.start + y1, from_y.size)
            send(field.at[from_x, from_y], field.at[to_x, to_y], dx, dy, group)

    def block_2(field, dx, dy):
        return field.at[pl.ds(5 + 2 * dx, 2), pl.ds(y2 + 8 * dy, 8)]

    def send_2(field, group, corners):
        for dx, dy in far:
            if corners or abs(dx) + abs(dy) < 4:
                send(block_2(field, 0, 0), block_2(field, -dx, -dy), dx, dy, group)

    ring = nx == 4
    wrap_2 = (lambda x: (x - 1) % 8 + 1) if ring else same
    wrap_3 = (lambda x: (x - 1) % 2 + 1) if ring else same
    planes_1 = range(1, 15)
    inner_1 = range(2, 14)
    planes_2 = range(1, 9) if ring else range(1, 11)
    planes_3 = range(1, 3) if ring else range(1, 4)
    limit = 8 if ring else 10

    send_0(1, 0, 4, X_0)
    send_0(-1, 0, 4, X_0)
    send_0(0, 1, 5, Y_0)
    send_0(0, -1, 5, Y_0)
    for dx in (1, -1):
        for dy in (1, -1):
            send_0(dx, dy, 4, X_0)


    def fold(first, count):
        plane = residual_plane(w0, f0, c0, d0, y0, 16)
        restrict(0, plane, f1, tmp, 5 + 4 * first, count, 16, 4 + first, y1)

    sweep(7, 35, u0, v0, f0, c0, g0, (y0 + 2, OWN - 4))
    sweep(8, 34, v0, w0, f0, c0, g0, (y0 + 3, OWN - 6))
    send_1(b1, B_1)
    for dx in (1, -1):
        send_0(dx, 0, 5, OUTER, 1)
    arrive(Y_0)
    for at in (1, 33):
        build(0, range(6, 36), same, b0, *c0, d0, g0, f0, u0, (at, 8))
    for at in (2, 32):
        sweep(7, 35, u0, v0, f0, c0, g0, (at, 8))
    for at in (3, 31):
        sweep(8, 34, v0, w0, f0, c0, g0, (at, 8))
    fold(1, 6)
    arrive(X_0)
    build(0, range(2, 6), same, b0, *c0, d0, g0, f0, u0)
    build(0, range(36, 40), same, b0, *c0, d0, g0, f0, u0)
    sweep(3, 7, u0, v0, f0, c0, g0)
    sweep(35, 39, u0, v0, f0, c0, g0)
    sweep(4, 8, v0, w0, f0, c0, g0)
    sweep(34, 38, v0, w0, f0, c0, g0)
    fold(0, 1)
    fold(7, 1)
    send_1(f1, F_1)
    send_2(b2, B_2, True)
    arrive(B_1)
    build(1, planes_1, same, b1, *c1, d1, g1)
    arrive(OUTER)
    build(0, range(1, 2), same, b0, *c0, d0, g0, f0, u0)
    build(0, range(40, 41), same, b0, *c0, d0, g0, f0, u0)
    for x in (2, 39):
        sweep(x, x + 1, u0, v0, f0, c0, g0)
    for x in (3, 38):
        sweep(x, x + 1, v0, w0, f0, c0, g0)
    arrive(F_1)

    first_sweep(1, planes_1, u1, f1, g1)
    sweep_packed(1, inner_1, same, u1, v1, f1, c1, g1)
    sweep_packed(1, inner_1, same, v1, u1, f1, c1, g1)
    restrict(1, residual_packed(1, same, u1, f1, c1, d1, y1, 8), f2, tmp, 4, 2, 8, 5, y2)
    send_2(f2, F_2, False)
    arrive(B_2)
    restrict(2, field_plane(b2, 0, 20), b3, tmp, 1, len(planes_3), 20, 1, 0, limit)
    build(2, planes_2, wrap_2, b2, *c2, d2, g2)
    build(3, planes_3, wrap_3, b3, *c3, d3, g3)
    arrive(F_2)

    first_sweep(2, planes_2, u2, f2, g2)
    sweep_packed(2, planes_2, wrap_2, u2, v2, f2, c2, g2)
    sweep_packed(2, planes_2, wrap_2, v2, u2, f2, c2, g2)
    restrict(
        2, residual_packed(2, wrap_2, u2, f2, c2, d2, 4, 16), f3, tmp, 1, len(planes_3), 16, 1, 2, limit
    )

    first_sweep(3, planes_3, u3, f3, g3)
    for _ in range(2):
        sweep_packed(3, planes_3, wrap_3, u3, v3, f3, c3, g3)
        sweep_packed(3, planes_3, wrap_3, v3, u3, f3, c3, g3)

    add_coarse(2, u2, u3, tmp, 1, 3, 1, y3 - 2, y2 - 4, 8, (4, 5, 6, 7))
    middle = (y2 - 4, 16)
    sweep_packed(2, range(4, 8), same, u2, v2, f2, c2, g2, middle)
    sweep_packed(2, range(4, 8), same, v2, u2, f2, c2, g2, middle)

    add_coarse(1, u1, u2, tmp, 4, 8, 0, y2 - 2, y1 - 4, 12, inner_1)
    sweep_packed(1, range(3, 13), same, u1, v1, f1, c1, g1)
    sweep_packed(1, range(3, 13), same, v1, u1, f1, c1, g1)

    add_coarse(0, w0, u1, tmp, 3, 13, 1, y1 - 2, 1, 20)
    sweep(4, 38, w0, v0, f0, c0, g0)

    own = pl.ds(y0, OWN)

    def last(x):
        here, total = gather(x, v0, *c0, y0, OWN)
        out[x - 5] = (1.0 - OMEGA) * here + g0[x, own] * (f0[x, own] + total)

    loop(5, 37, last, 16)
    settle(send_sem, 0, sum(sizes.values()))


def solution(mesh):
    nx, ny = mesh.shape["gx"], mesh.shape["gy"]
    shapes = []
    for planes, height in zip(PLANES, ROWS):
        shapes += [pltpu.VMEM((planes, height + 8, 128), F32)] + [pltpu.VMEM((planes, height, 128), F32)] * 10

    def per_device(source, inverse_density):
        return pl.pallas_call(
            functools.partial(kernel, nx, ny),
            out_shape=jax.ShapeDtypeStruct(source.shape, F32),
            in_specs=[pl.BlockSpec(memory_space=pl.ANY)] * 2,
            out_specs=pl.BlockSpec(memory_space=pltpu.VMEM),
            scratch_shapes=shapes
            + [
                pltpu.VMEM((20, 48, 128), F32),
                pltpu.SemaphoreType.DMA((2,)),
                pltpu.SemaphoreType.DMA((1,)),
                pltpu.SemaphoreType.DMA((7,)),
                pltpu.VMEM((5120, 128), F32),
            ],
            compiler_params=pltpu.CompilerParams(
                collective_id=0, has_side_effects=True, vmem_limit_bytes=40 * 2**20
            ),
        )(source, inverse_density)

    placed = (P("gx", "gy", None), P("gx", "gy", None))
    return jax.shard_map(
        per_device, mesh=mesh, in_specs=placed, out_specs=P("gx", "gy", None), check_vma=False
    )
```
